128 devices in a mesh: expert: 8 (over x, core), tensor: 16 (over y, z).
Axes of the slice: x: 4, y: 4, z: 4, core: 2. Of those that a mesh axis runs over, the one named last changes fastest.
Arguments:
- tokens: bfloat16 [16384, 2048], P(('expert', 'tensor')), may hold values from -6 to 6
- expert_ids: int32 [16384, 8], P(('expert', 'tensor')), may hold values from 0 to 127, all different within a row; in each aligned block of 128 rows (0 to 127, 128 to 255, ...) at most 16 rows name the same one
- route_gates: float32 [16384, 8], P(('expert', 'tensor')), may hold values from 0.05 to 0.45
- expert_weights: bfloat16 [128, 3, 768, 2048], P('expert', None, 'tensor'), may hold values from -0.125 to 0.125
Outputs:
- combined: bfloat16 [16384, 2048], P(('expert', 'tensor'))
The draws below stay inside these ranges and needn't reach their ends.
Inputs may be any that keep to these rules, and one draw needn't show every extreme that they name: `expert_ids`: each row names 8 different experts; within the 128 rows of one device (aligned blocks) no expert is named by more than 16 rows, a bound that some block reaches.
All inputs are finite; a program needn't handle non-finite values.
Results may differ from the reference program's by a relative error of at most 0.015.
Values may be sent and summed in bfloat16 or wider, within the bound.
No kernel may reach another device: no remote copies, remote signals or barrier semaphores. Data moves between devices by JAX's collectives and lax.ppermute only.
A program may use at most 192 MiB of HBM per device.

```python
import math
import jax
import jax.numpy as jnp
import numpy as np
from jax import lax

D = 2048
FF = 768
TOPK = 8
TOK_DEV = 128
E = 128
MOST = 16
FB = 48
TOKENS = 16384
N_EXPERT = 8
N_TENSOR = 16


def block_levels(stream_key, shape, shards, low, top_value):
    def one(dim, blocks):
        draws = jax.random.uniform(jax.random.fold_in(jax.random.fold_in(stream_key, 6), dim), (blocks,), jnp.float32, low / len(shards), top_value / len(shards))
        return jnp.repeat(jnp.exp(draws), shape[dim] // blocks).reshape((-1,) + (1,) * (len(shape) - dim - 1))

    gain = one(*shards[0])
    for cut in shards[1:]:
        gain = gain * one(*cut)
    return gain


def routed_block(own_key, own, number, rows, number_of, top, most, lean):
    ranking = jax.random.permutation(own_key, number_of)
    crowded, usual = portions_of(number_of, rows * top, most, lean, True), portions_of(number_of, rows * top, most, lean, False)
    places = jnp.arange(number_of)

    def named(tallies, rotation):
        used = int((tallies > 0).sum())
        fixed = max(1, used // 4)
        passed = fixed + (places - fixed + rotation * (used - fixed)) % max(1, number_of - fixed)
        return jnp.zeros((number_of,), jnp.int32).at[ranking[jnp.where(places < fixed, places, passed)]].set(jnp.asarray(tallies, jnp.int32))

    tallies = jnp.where(number % 4 == 0, named(crowded, number // 4), named(usual, number - number // 4 - 1))
    mixed = jax.random.permutation(jax.random.fold_in(own, 3), number_of)
    giver, sink = mixed[0:number_of // 2 * 2:2], mixed[1:number_of // 2 * 2:2]
    room = jnp.minimum(tallies[giver] - 1, most - tallies[sink]) // 2
    room = jnp.where((giver == ranking[0]) | (sink == ranking[0]) | (tallies[sink] == 0), 0, jnp.maximum(room, 0))
    passed = jax.random.randint(jax.random.fold_in(own, 4), (number_of // 2,), 0, 1 << 20) % (room + 1)
    tallies = tallies.at[giver].add(-passed).at[sink].add(passed)
    labels = jnp.searchsorted(jnp.cumsum(tallies), jnp.arange(rows * top), side="right").astype(jnp.int32)
    listing = labels.reshape(top, rows).T
    listing = listing[jax.random.permutation(jax.random.fold_in(own, 1), rows)]
    rotation = jax.random.randint(jax.random.fold_in(own, 2), (rows, 1), 0, top)
    return jnp.take_along_axis(listing, (jnp.arange(top)[None, :] + rotation) % top, axis=1)


def portions_of(count, total, most, lean, full):
    weights = [(1 << 20) // math.isqrt(rank ** lean) + 1 for rank in range(1, count + 1)]
    largest = most if full else min(most, max(-(-total // count), total * weights[0] // sum(weights)))
    least = 1 if total - largest >= count - 1 else 0
    given, spare = [largest] + [least] * (count - 1), total - largest - least * (count - 1)
    while spare > 0:
        free = [i for i in range(1, count) if given[i] < largest] or [i for i in range(1, count) if given[i] < most]
        pool, left = sum([weights[i] for i in free]), spare
        for i in free:
            extra = min(most - given[i], max(1, left * weights[i] // pool), spare)
            given[i] = given[i] + extra
            spare = spare - extra
    return np.array(given)


def noise(rng, dims, width, most, split=(), kind=jnp.bfloat16):
    loudness = block_levels(rng, dims, split, -0.22, 0.18) if split else 1.0
    array = jax.random.normal(rng, dims, jnp.float32) * width * loudness
    return jnp.minimum(jnp.maximum(array, -most), most).astype(kind)


def setup_inputs(seed: int = 0) -> dict:
    seeds = jax.random.split(jax.random.key(seed), 5)
    tokens = noise(seeds[0], (TOKENS, D), 1.0, 6.0, ((0, 128),))
    expert_ids_keys = jax.random.split(jax.random.fold_in(seeds[1], 1), TOKENS // TOK_DEV)
    expert_ids_turns = jax.random.permutation(jax.random.fold_in(seeds[1], 3), TOKENS // TOK_DEV)
    expert_ids = jax.vmap(lambda own, number: routed_block(jax.random.fold_in(seeds[1], 2), own, number, TOK_DEV, E, TOPK, MOST, 1))(expert_ids_keys, expert_ids_turns).reshape((TOKENS, TOPK))
    route_gates = jnp.clip(0.05 + 0.39999999 * jax.random.uniform(seeds[2], (TOKENS, TOPK), jnp.float32) ** block_levels(seeds[2], (TOKENS, TOPK), ((0, 128),), -0.2, 0.2), 0.05, 0.45)
    expert_weights = noise(seeds[3], (E, 3, FF, D), D ** -0.5, 0.125, ((0, 8), (2, 16)))
    return {"tokens": tokens, "expert_ids": expert_ids, "route_gates": route_gates, "expert_weights": expert_weights}


def reference(tokens, expert_ids, route_gates, expert_weights):
    devices = N_EXPERT * N_TENSOR
    pairs = TOK_DEV * TOPK
    grouped = expert_ids.reshape(devices, pairs).astype(jnp.int32)
    onehot = (grouped[:, :, None] == jnp.arange(E, dtype=jnp.int32)[None, None, :]).astype(jnp.int32)
    earlier = (jnp.cumsum(onehot, axis=1).astype(jnp.int32) - onehot) * onehot
    ranked = jnp.sum(earlier, axis=2).astype(jnp.int32)
    device_index = jnp.arange(devices, dtype=jnp.int32)[:, None]
    position = (device_index * MOST + ranked).reshape(-1).astype(jnp.int32)
    flat_ids = grouped.reshape(-1)
    token_index = (jnp.arange(devices * pairs, dtype=jnp.int32) // TOPK).astype(jnp.int32)
    buffer = jnp.zeros((E, devices * MOST, D), jnp.bfloat16)
    buffer = buffer.at[flat_ids, position].set(tokens[token_index])

    def expert_fn(operand):
        expert_rows, weights = operand
        gate = jnp.dot(expert_rows, weights[0].T, preferred_element_type=jnp.float32)
        up_proj = jnp.dot(expert_rows, weights[1].T, preferred_element_type=jnp.float32)
        hidden = (jax.nn.silu(gate) * up_proj).astype(jnp.bfloat16)
        blocks = FF // FB
        hidden_blocks = hidden.reshape(expert_rows.shape[0], blocks, FB).astype(jnp.float32)
        down_blocks = weights[2].reshape(blocks, FB, D).astype(jnp.float32)
        block_sum = jnp.einsum("rbf,bfd->brd", hidden_blocks, down_blocks).astype(jnp.bfloat16)
        return jnp.sum(block_sum.astype(jnp.float32), axis=0).astype(jnp.bfloat16)

    outputs = lax.map(expert_fn, (buffer, expert_weights))
    picked = outputs[flat_ids, position].astype(jnp.float32).reshape(TOKENS, TOPK, D)
    combined = jnp.sum(route_gates.astype(jnp.float32)[:, :, None] * picked, axis=1)
    return combined.astype(jnp.bfloat16)
```

```python
import jax
import jax.numpy as jnp
from jax import lax
from jax.experimental import pallas as pl
from jax.experimental.pallas import tpu as pltpu
from jax.sharding import PartitionSpec as P

MOST = 16
AXES = ("expert", "tensor")


def slot_codes(ids_t, experts):
    top, rows = ids_t.shape
    names = lax.broadcasted_iota(jnp.int32, (experts, rows), 0)
    member = names == ids_t[0:1, :]
    for k in range(1, top):
        member = member | (names == ids_t[k : k + 1, :])
    before = lax.broadcasted_iota(jnp.int32, (rows, rows), 0) < lax.broadcasted_iota(
        jnp.int32, (rows, rows), 1
    )
    rank = jnp.dot(
        member.astype(jnp.float32).astype(jnp.bfloat16),
        before.astype(jnp.float32).astype(jnp.bfloat16),
        preferred_element_type=jnp.float32,
    )
    return jnp.where(member, rank, -1.0)


def dispatch_kernel(ids_ref, tokens_ref, out_ref, code_ref):
    part = out_ref.shape[0]
    step = pl.program_id(0)

    @pl.when(step == 0)
    def _():
        code_ref[...] = slot_codes(ids_ref[...], code_ref.shape[0])

    code = code_ref[pl.ds(pl.multiple_of(step * part, part), part), :]
    rows = code.shape[1]
    slots = lax.broadcasted_iota(jnp.int32, (part, MOST, rows), 1).astype(jnp.float32)
    pick = jnp.where(code[:, None, :] == slots, 1.0, 0.0)
    pick = pick.reshape(part * MOST, rows).astype(jnp.bfloat16)
    picked = jnp.dot(pick, tokens_ref[...], preferred_element_type=jnp.float32)
    out_ref[...] = picked.astype(jnp.bfloat16).reshape(out_ref.shape)


def dispatch(ids_t, tokens, experts):
    rows, width = tokens.shape
    part = 16
    return pl.pallas_call(
        dispatch_kernel,
        out_shape=jax.ShapeDtypeStruct((experts, MOST, width), jnp.bfloat16),
        grid=(experts // part,),
        in_specs=[
            pl.BlockSpec(ids_t.shape, lambda i: (0, 0)),
            pl.BlockSpec((rows, width), lambda i: (0, 0)),
        ],
        out_specs=pl.BlockSpec((part, MOST, width), lambda i: (i, 0, 0)),
        scratch_shapes=[pltpu.VMEM((experts, rows), jnp.float32)],
        compiler_params=pltpu.CompilerParams(vmem_limit_bytes=32 << 20),
        cost_estimate=pl.CostEstimate(
            flops=2 * experts * MOST * rows * width,
            bytes_accessed=2 * (experts * MOST + rows) * width,
            transcendentals=0,
        ),
        name="dispatch",
    )(ids_t, tokens)


def ffn_kernel(rows_ref, weights_ref, out_ref):
    blocks, _, width_block, model = weights_ref.shape
    hidden_units = blocks * width_block
    contract_last = (((1,), (1,)), ((), ()))
    x = rows_ref[...]
    w_gate = weights_ref[:, 0].reshape(hidden_units, model)
    w_up = weights_ref[:, 1].reshape(hidden_units, model)
    w_down = weights_ref[:, 2].reshape(hidden_units, model)
    gate = lax.dot_general(x, w_gate, contract_last, preferred_element_type=jnp.float32)
    up = lax.dot_general(x, w_up, contract_last, preferred_element_type=jnp.float32)
    hidden = (gate / (1.0 + jnp.exp(-gate)) * up).astype(jnp.bfloat16)
    out_ref[...] = jnp.dot(hidden, w_down, preferred_element_type=jnp.float32).astype(jnp.bfloat16)


def expert_ffn(rows, weights):
    count, model = rows.shape
    part = 256
    return pl.pallas_call(
        ffn_kernel,
        out_shape=jax.ShapeDtypeStruct((count, model), jnp.bfloat16),
        grid=(count // part,),
        in_specs=[
            pl.BlockSpec((part, model), lambda i: (i, 0)),
            pl.BlockSpec(weights.shape, lambda i: (0, 0, 0, 0), pipeline_mode=pl.Buffered(1)),
        ],
        out_specs=pl.BlockSpec((part, model), lambda i: (i, 0)),
        compiler_params=pltpu.CompilerParams(vmem_limit_bytes=48 << 20),
        cost_estimate=pl.CostEstimate(
            flops=2 * count * weights.size,
            bytes_accessed=2 * (2 * rows.size + weights.size),
            transcendentals=count * weights.size // (3 * model),
        ),
        name="expert_ffn",
    )(rows, weights)


def combine_kernel(ids_ref, gates_ref, rows_ref, out_ref, total_ref, code_ref, gate_ref):
    part = rows_ref.shape[0]
    step = pl.program_id(0)

    @pl.when(step == 0)
    def _():
        ids_t = ids_ref[...]
        experts, rows = code_ref.shape
        code_ref[...] = slot_codes(ids_t, experts)
        names = lax.broadcasted_iota(jnp.int32, (experts, rows), 0)
        gate = jnp.zeros((experts, rows), jnp.float32)
        for k in range(ids_t.shape[0]):
            gate = jnp.where(names == ids_t[k : k + 1, :], gates_ref[k : k + 1, :], gate)
        gate_ref[...] = gate
        total_ref[...] = jnp.zeros_like(total_ref)

    here = pl.ds(pl.multiple_of(step * part, part), part)
    code = code_ref[here, :]
    gate = gate_ref[here, :]
    rows = code.shape[1]
    slots = lax.broadcasted_iota(jnp.int32, (part, MOST, rows), 1).astype(jnp.float32)
    weight = jnp.where(code[:, None, :] == slots, gate[:, None, :], 0.0)
    weight = weight.reshape(part * MOST, rows)
    high = weight.astype(jnp.bfloat16)
    low = (weight - high.astype(jnp.float32)).astype(jnp.bfloat16)
    both = jnp.concatenate([high, low], axis=1)
    values = rows_ref[...].reshape(part * MOST, rows_ref.shape[2])
    sums = lax.dot_general(
        both, values, (((0,), (0,)), ((), ())), preferred_element_type=jnp.float32
    )
    total_ref[...] += sums[:rows] + sums[rows:]

    @pl.when(step == pl.num_programs(0) - 1)
    def _():
        out_ref[...] = total_ref[...].astype(jnp.bfloat16)


def combine(ids_t, gates_t, returned):
    experts, most, width = returned.shape
    rows = ids_t.shape[1]
    part = 16
    return pl.pallas_call(
        combine_kernel,
        out_shape=jax.ShapeDtypeStruct((rows, width), jnp.bfloat16),
        grid=(experts // part,),
        in_specs=[
            pl.BlockSpec(ids_t.shape, lambda i: (0, 0)),
            pl.BlockSpec(gates_t.shape, lambda i: (0, 0)),
            pl.BlockSpec((part, most, width), lambda i: (i, 0, 0)),
        ],
        out_specs=pl.BlockSpec((rows, width), lambda i: (0, 0)),
        scratch_shapes=[
            pltpu.VMEM((rows, width), jnp.float32),
            pltpu.VMEM((experts, rows), jnp.float32),
            pltpu.VMEM((experts, rows), jnp.float32),
        ],
        compiler_params=pltpu.CompilerParams(vmem_limit_bytes=32 << 20),
        cost_estimate=pl.CostEstimate(
            flops=4 * experts * most * rows * width,
            bytes_accessed=2 * (experts * most + rows) * width,
            transcendentals=0,
        ),
        name="combine",
    )(ids_t, gates_t, returned)


def body(tokens, expert_ids, route_gates, expert_weights):
    groups = lax.axis_size("expert")
    experts = expert_weights.shape[0] * groups
    model = tokens.shape[1]
    ids_t = expert_ids.T
    gates_t = route_gates.T
    weights = lax.all_to_all(expert_weights, "tensor", split_axis=0, concat_axis=0, tiled=True)
    outgoing = dispatch(ids_t, tokens, experts)
    arrived = lax.all_to_all(outgoing, AXES, split_axis=0, concat_axis=0, tiled=True)
    outputs = expert_ffn(arrived.reshape(experts * MOST, model), weights)
    returned = lax.all_to_all(
        outputs.reshape(experts, MOST, model), AXES, split_axis=0, concat_axis=0, tiled=True
    )
    return combine(ids_t, gates_t, returned)


def solution(mesh):
    in_specs = (
        P(AXES, None),
        P(AXES, None),
        P(AXES, None),
        P("expert", None, "tensor", None),
    )
    return jax.shard_map(
        body, mesh=mesh, in_specs=in_specs, out_specs=P(AXES, None), check_vma=False
    )
```

```python
import functools

import jax
import jax.numpy as jnp
from jax import lax
from jax.experimental import pallas as pl
from jax.experimental.pallas import tpu as pltpu
from jax.sharding import PartitionSpec as P

MOST = 16
AXES = ("expert", "tensor")


def slot_codes(ids_t, experts):
    top, rows = ids_t.shape
    names = lax.broadcasted_iota(jnp.int32, (experts, rows), 0)
    member = names == ids_t[0:1, :]
    for k in range(1, top):
        member = member | (names == ids_t[k : k + 1, :])
    before = lax.broadcasted_iota(jnp.int32, (rows, rows), 0) < lax.broadcasted_iota(
        jnp.int32, (rows, rows), 1
    )
    rank = jnp.dot(
        member.astype(jnp.float32).astype(jnp.bfloat16),
        before.astype(jnp.float32).astype(jnp.bfloat16),
        preferred_element_type=jnp.float32,
    )
    return jnp.where(member, rank, -1.0)


def dispatch_kernel(ids_ref, tokens_ref, *refs):
    code_ref = refs[-1]
    out_refs = refs[:-1]
    part = out_refs[0].shape[0]
    step = pl.program_id(0)

    @pl.when(step == 0)
    def _():
        code_ref[...] = slot_codes(ids_ref[...], code_ref.shape[0])

    code = code_ref[pl.ds(pl.multiple_of(step * part, part), part), :]
    rows = code.shape[1]
    first = 0
    for out_ref in out_refs:
        count = out_ref.shape[1]
        slots = first + lax.broadcasted_iota(jnp.int32, (part, count, rows), 1)
        pick = jnp.where(code[:, None, :] == slots.astype(jnp.float32), 1.0, 0.0)
        pick = pick.reshape(part * count, rows).astype(jnp.bfloat16)
        picked = jnp.dot(pick, tokens_ref[...], preferred_element_type=jnp.float32)
        out_ref[...] = picked.reshape(out_ref.shape).astype(jnp.bfloat16)
        first += count


def dispatch(ids_t, tokens, experts, counts):
    rows, width = tokens.shape
    part = 16
    return pl.pallas_call(
        dispatch_kernel,
        out_shape=[jax.ShapeDtypeStruct((experts, n, width), jnp.bfloat16) for n in counts],
        grid=(experts // part,),
        in_specs=[
            pl.BlockSpec(ids_t.shape, lambda i: (0, 0)),
            pl.BlockSpec((rows, width), lambda i: (0, 0)),
        ],
        out_specs=[pl.BlockSpec((part, n, width), lambda i: (i, 0, 0)) for n in counts],
        scratch_shapes=[pltpu.VMEM((experts, rows), jnp.float32)],
        compiler_params=pltpu.CompilerParams(vmem_limit_bytes=32 << 20),
        cost_estimate=pl.CostEstimate(
            flops=2 * experts * MOST * rows * width,
            bytes_accessed=2 * (experts * MOST + rows) * width,
            transcendentals=0,
        ),
        name="dispatch",
    )(ids_t, tokens)


def ffn_kernel(rows_ref, weights_ref, out_ref):
    blocks, _, width_block, model = weights_ref.shape
    hidden_units = blocks * width_block
    contract_last = (((1,), (1,)), ((), ()))
    x = rows_ref[...]
    w_gate = weights_ref[:, 0].reshape(hidden_units, model)
    w_up = weights_ref[:, 1].reshape(hidden_units, model)
    w_down = weights_ref[:, 2].reshape(hidden_units, model)
    gate = lax.dot_general(x, w_gate, contract_last, preferred_element_type=jnp.float32)
    up = lax.dot_general(x, w_up, contract_last, preferred_element_type=jnp.float32)
    hidden = (gate / (1.0 + jnp.exp(-gate)) * up).astype(jnp.bfloat16)
    out_ref[...] = jnp.dot(hidden, w_down, preferred_element_type=jnp.float32).astype(jnp.bfloat16)


def expert_ffn(rows, weights):
    count, model = rows.shape
    part = 256
    return pl.pallas_call(
        ffn_kernel,
        out_shape=jax.ShapeDtypeStruct((count, model), jnp.bfloat16),
        grid=(count // part,),
        in_specs=[
            pl.BlockSpec((part, model), lambda i: (i, 0)),
            pl.BlockSpec(weights.shape, lambda i: (0, 0, 0, 0), pipeline_mode=pl.Buffered(1)),
        ],
        out_specs=pl.BlockSpec((part, model), lambda i: (i, 0)),
        compiler_params=pltpu.CompilerParams(vmem_limit_bytes=48 << 20),
        cost_estimate=pl.CostEstimate(
            flops=2 * count * weights.size,
            bytes_accessed=2 * (2 * rows.size + weights.size),
            transcendentals=count * weights.size // (3 * model),
        ),
        name="expert_ffn",
    )(rows, weights)


def combine_kernel(first, ids_ref, gates_ref, rows_ref, *refs):
    *start_refs, out_ref, total_ref, code_ref, gate_ref = refs
    part, count, width = rows_ref.shape
    step = pl.program_id(0)

    @pl.when(step == 0)
    def _():
        ids_t = ids_ref[...]
        experts, rows = code_ref.shape
        code_ref[...] = slot_codes(ids_t, experts)
        names = lax.broadcasted_iota(jnp.int32, (experts, rows), 0)
        gate = jnp.zeros((experts, rows), jnp.float32)
        for k in range(ids_t.shape[0]):
            gate = jnp.where(names == ids_t[k : k + 1, :], gates_ref[k : k + 1, :], gate)
        gate_ref[...] = gate
        total_ref[...] = start_refs[0][...] if start_refs else jnp.zeros_like(total_ref)

    here = pl.ds(pl.multiple_of(step * part, part), part)
    code = code_ref[here, :]
    gate = gate_ref[here, :]
    rows = code.shape[1]
    slots = first + lax.broadcasted_iota(jnp.int32, (part, count, rows), 1)
    weight = jnp.where(code[:, None, :] == slots.astype(jnp.float32), gate[:, None, :], 0.0)
    weight = weight.reshape(part * count, rows)
    high = weight.astype(jnp.bfloat16)
    low = (weight - high.astype(jnp.float32)).astype(jnp.bfloat16)
    both = jnp.concatenate([high, low], axis=1)
    values = rows_ref[...].reshape(part * count, width)
    sums = lax.dot_general(
        both, values, (((0,), (0,)), ((), ())), preferred_element_type=jnp.float32
    )
    total_ref[...] += sums[:rows] + sums[rows:]

    @pl.when(step == pl.num_programs(0) - 1)
    def _():
        out_ref[...] = total_ref[...].astype(out_ref.dtype)


def combine(ids_t, gates_t, returned, first, start, dtype):
    experts, count, width = returned.shape
    rows = ids_t.shape[1]
    part = 16
    whole = pl.BlockSpec((rows, width), lambda i: (0, 0))
    return pl.pallas_call(
        functools.partial(combine_kernel, first),
        out_shape=jax.ShapeDtypeStruct((rows, width), dtype),
        grid=(experts // part,),
        in_specs=[
            pl.BlockSpec(ids_t.shape, lambda i: (0, 0)),
            pl.BlockSpec(gates_t.shape, lambda i: (0, 0)),
            pl.BlockSpec((part, count, width), lambda i: (i, 0, 0)),
        ]
        + [whole] * len(start),
        out_specs=whole,
        scratch_shapes=[
            pltpu.VMEM((rows, width), jnp.float32),
            pltpu.VMEM((experts, rows), jnp.float32),
            pltpu.VMEM((experts, rows), jnp.float32),
        ],
        compiler_params=pltpu.CompilerParams(vmem_limit_bytes=32 << 20),
        cost_estimate=pl.CostEstimate(
            flops=4 * experts * count * rows * width,
            bytes_accessed=2 * (experts * count + rows) * width,
            transcendentals=0,
        ),
        name="combine",
    )(ids_t, gates_t, returned, *start)


def exchange(rows):
    return lax.all_to_all(rows, AXES, split_axis=0, concat_axis=0, tiled=True)


def body(tokens, expert_ids, route_gates, expert_weights):
    groups = lax.axis_size("expert")
    experts = expert_weights.shape[0] * groups
    model = tokens.shape[1]
    ids_t = expert_ids.T
    gates_t = route_gates.T
    half = MOST // 2
    weights = lax.all_to_all(expert_weights, "tensor", split_axis=0, concat_axis=0, tiled=True)
    out_a, out_b = dispatch(ids_t, tokens, experts, (half, half))
    out_a, out_b, weights = lax.optimization_barrier((out_a, out_b, weights))
    in_a = exchange(out_a)
    in_a, out_b = lax.optimization_barrier((in_a, out_b))
    in_b = exchange(out_b)
    done_a = expert_ffn(in_a.reshape(experts * half, model), weights)
    done_a, in_b = lax.optimization_barrier((done_a, in_b))
    back_a = exchange(done_a.reshape(experts, half, model))
    done_b = expert_ffn(in_b.reshape(experts * half, model), weights)
    done_b, back_a = lax.optimization_barrier((done_b, back_a))
    back_b = exchange(done_b.reshape(experts, half, model))
    part = combine(ids_t, gates_t, back_a, 0, (), jnp.float32)
    return combine(ids_t, gates_t, back_b, half, (part,), jnp.bfloat16)


def solution(mesh):
    in_specs = (
        P(AXES, None),
        P(AXES, None),
        P(AXES, None),
        P("expert", None, "tensor", None),
    )
    return jax.shard_map(
        body, mesh=mesh, in_specs=in_specs, out_specs=P(AXES, None), check_vma=False
    )
```

```python
import functools

import jax
import jax.numpy as jnp
from jax import lax
from jax.experimental import pallas as pl
from jax.experimental.pallas import tpu as pltpu
from jax.sharding import PartitionSpec as P

MOST = 16
AXES = ("expert", "tensor")


def slot_codes(ids_t, experts):
    top, rows = ids_t.shape
    names = lax.broadcasted_iota(jnp.int32, (experts, rows), 0)
    member = names == ids_t[0:1, :]
    for k in range(1, top):
        member = member | (names == ids_t[k : k + 1, :])
    before = lax.broadcasted_iota(jnp.int32, (rows, rows), 0) < lax.broadcasted_iota(
        jnp.int32, (rows, rows), 1
    )
    rank = jnp.dot(
        member.astype(jnp.float32).astype(jnp.bfloat16),
        before.astype(jnp.float32).astype(jnp.bfloat16),
        preferred_element_type=jnp.float32,
    )
    return jnp.where(member, rank, -1.0)


def dispatch_kernel(ids_ref, tokens_ref, *refs):
    code_ref = refs[-1]
    out_refs = refs[:-1]
    part = out_refs[0].shape[0]
    step = pl.program_id(0)

    @pl.when(step == 0)
    def _():
        code_ref[...] = slot_codes(ids_ref[...], code_ref.shape[0])

    code = code_ref[pl.ds(pl.multiple_of(step * part, part), part), :]
    rows = code.shape[1]
    first = 0
    for out_ref in out_refs:
        count = out_ref.shape[1]
        slots = first + lax.broadcasted_iota(jnp.int32, (part, count, rows), 1)
        pick = jnp.where(code[:, None, :] == slots.astype(jnp.float32), 1.0, 0.0)
        pick = pick.reshape(part * count, rows).astype(jnp.bfloat16)
        picked = jnp.dot(pick, tokens_ref[...], preferred_element_type=jnp.float32)
        out_ref[...] = picked.reshape(out_ref.shape).astype(jnp.bfloat16)
        first += count


def dispatch(ids_t, tokens, experts, counts):
    rows, width = tokens.shape
    part = 16
    return pl.pallas_call(
        dispatch_kernel,
        out_shape=[jax.ShapeDtypeStruct((experts, n, width), jnp.bfloat16) for n in counts],
        grid=(experts // part,),
        in_specs=[
            pl.BlockSpec(ids_t.shape, lambda i: (0, 0)),
            pl.BlockSpec((rows, width), lambda i: (0, 0)),
        ],
        out_specs=[pl.BlockSpec((part, n, width), lambda i: (i, 0, 0)) for n in counts],
        scratch_shapes=[pltpu.VMEM((experts, rows), jnp.float32)],
        compiler_params=pltpu.CompilerParams(vmem_limit_bytes=32 << 20),
        cost_estimate=pl.CostEstimate(
            flops=2 * experts * MOST * rows * width,
            bytes_accessed=2 * (experts * MOST + rows) * width,
            transcendentals=0,
        ),
        name="dispatch",
    )(ids_t, tokens)


def ffn_kernel(rows_ref, weights_ref, out_ref):
    blocks, _, width_block, model = weights_ref.shape
    hidden_units = blocks * width_block
    contract_last = (((1,), (1,)), ((), ()))
    x = rows_ref[...]
    w_gate = weights_ref[:, 0].reshape(hidden_units, model)
    w_up = weights_ref[:, 1].reshape(hidden_units, model)
    w_down = weights_ref[:, 2].reshape(hidden_units, model)
    gate = lax.dot_general(x, w_gate, contract_last, preferred_element_type=jnp.float32)
    up = lax.dot_general(x, w_up, contract_last, preferred_element_type=jnp.float32)
    hidden = (gate / (1.0 + jnp.exp(-gate)) * up).astype(jnp.bfloat16)
    out_ref[...] = jnp.dot(hidden, w_down, preferred_element_type=jnp.float32).astype(jnp.bfloat16)


def expert_ffn(rows, weights):
    count, model = rows.shape
    part = 256
    return pl.pallas_call(
        ffn_kernel,
        out_shape=jax.ShapeDtypeStruct((count, model), jnp.bfloat16),
        grid=(count // part,),
        in_specs=[
            pl.BlockSpec((part, model), lambda i: (i, 0)),
            pl.BlockSpec(weights.shape, lambda i: (0, 0, 0, 0), pipeline_mode=pl.Buffered(1)),
        ],
        out_specs=pl.BlockSpec((part, model), lambda i: (i, 0)),
        compiler_params=pltpu.CompilerParams(vmem_limit_bytes=48 << 20),
        cost_estimate=pl.CostEstimate(
            flops=2 * count * weights.size,
            bytes_accessed=2 * (2 * rows.size + weights.size),
            transcendentals=count * weights.size // (3 * model),
        ),
        name="expert_ffn",
    )(rows, weights)


def combine_kernel(first, ids_ref, gates_ref, rows_ref, *refs):
    *start_refs, out_ref, total_ref, code_ref, gate_ref = refs
    part, count, width = rows_ref.shape
    step = pl.program_id(0)

    @pl.when(step == 0)
    def _():
        ids_t = ids_ref[...]
        experts, rows = code_ref.shape
        code_ref[...] = slot_codes(ids_t, experts)
        names = lax.broadcasted_iota(jnp.int32, (experts, rows), 0)
        gate = jnp.zeros((experts, rows), jnp.float32)
        for k in range(ids_t.shape[0]):
            gate = jnp.where(names == ids_t[k : k + 1, :], gates_ref[k : k + 1, :], gate)
        gate_ref[...] = gate
        total_ref[...] = start_refs[0][...] if start_refs else jnp.zeros_like(total_ref)

    here = pl.ds(pl.multiple_of(step * part, part), part)
    code = code_ref[here, :]
    gate = gate_ref[here, :]
    rows = code.shape[1]
    slots = first + lax.broadcasted_iota(jnp.int32, (part, count, rows), 1)
    weight = jnp.where(code[:, None, :] == slots.astype(jnp.float32), gate[:, None, :], 0.0)
    weight = weight.reshape(part * count, rows)
    high = weight.astype(jnp.bfloat16)
    low = (weight - high.astype(jnp.float32)).astype(jnp.bfloat16)
    both = jnp.concatenate([high, low], axis=1)
    values = rows_ref[...].reshape(part * count, width)
    sums = lax.dot_general(
        both, values, (((0,), (0,)), ((), ())), preferred_element_type=jnp.float32
    )
    total_ref[...] += sums[:rows] + sums[rows:]

    @pl.when(step == pl.num_programs(0) - 1)
    def _():
        out_ref[...] = total_ref[...].astype(out_ref.dtype)


def combine(ids_t, gates_t, returned, first, start, dtype):
    experts, count, width = returned.shape
    rows = ids_t.shape[1]
    part = 16
    whole = pl.BlockSpec((rows, width), lambda i: (0, 0))
    return pl.pallas_call(
        functools.partial(combine_kernel, first),
        out_shape=jax.ShapeDtypeStruct((rows, width), dtype),
        grid=(experts // part,),
        in_specs=[
            pl.BlockSpec(ids_t.shape, lambda i: (0, 0)),
            pl.BlockSpec(gates_t.shape, lambda i: (0, 0)),
            pl.BlockSpec((part, count, width), lambda i: (i, 0, 0)),
        ]
        + [whole] * len(start),
        out_specs=whole,
        scratch_shapes=[
            pltpu.VMEM((rows, width), jnp.float32),
            pltpu.VMEM((experts, rows), jnp.float32),
            pltpu.VMEM((experts, rows), jnp.float32),
        ],
        compiler_params=pltpu.CompilerParams(vmem_limit_bytes=32 << 20),
        cost_estimate=pl.CostEstimate(
            flops=4 * experts * count * rows * width,
            bytes_accessed=2 * (experts * count + rows) * width,
            transcendentals=0,
        ),
        name="combine",
    )(ids_t, gates_t, returned, *start)


def exchange(rows):
    return lax.all_to_all(rows, AXES, split_axis=0, concat_axis=0, tiled=True)


def body(tokens, expert_ids, route_gates, expert_weights):
    groups = lax.axis_size("expert")
    experts = expert_weights.shape[0] * groups
    model = tokens.shape[1]
    ids_t = expert_ids.T
    gates_t = route_gates.T
    half = MOST // 2
    out_a, out_b = dispatch(ids_t, tokens, experts, (half, half))
    out_a, out_b, expert_weights = lax.optimization_barrier((out_a, out_b, expert_weights))
    weights = lax.all_to_all(expert_weights, "tensor", split_axis=0, concat_axis=0, tiled=True)
    out_a, out_b, weights = lax.optimization_barrier((out_a, out_b, weights))
    in_a = exchange(out_a)
    in_a, out_b = lax.optimization_barrier((in_a, out_b))
    in_b = exchange(out_b)
    done_a = expert_ffn(in_a.reshape(experts * half, model), weights)
    done_a, in_b = lax.optimization_barrier((done_a, in_b))
    back_a = exchange(done_a.reshape(experts, half, model))
    done_b = expert_ffn(in_b.reshape(experts * half, model), weights)
    done_b, back_a = lax.optimization_barrier((done_b, back_a))
    back_b = exchange(done_b.reshape(experts, half, model))
    part = combine(ids_t, gates_t, back_a, 0, (), jnp.float32)
    return combine(ids_t, gates_t, back_b, half, (part,), jnp.bfloat16)


def solution(mesh):
    in_specs = (
        P(AXES, None),
        P(AXES, None),
        P(AXES, None),
        P("expert", None, "tensor", None),
    )
    return jax.shard_map(
        body, mesh=mesh, in_specs=in_specs, out_specs=P(AXES, None), check_vma=False
    )
```

```python
import functools

import jax
import jax.numpy as jnp
from jax import lax
from jax.experimental import pallas as pl
from jax.experimental.pallas import tpu as pltpu
from jax.sharding import PartitionSpec as P

MOST = 16
AXES = ("expert", "tensor")


def slot_codes(ids_t, experts):
    top, rows = ids_t.shape
    names = lax.broadcasted_iota(jnp.int32, (experts, rows), 0)
    member = names == ids_t[0:1, :]
    for k in range(1, top):
        member = member | (names == ids_t[k : k + 1, :])
    before = lax.broadcasted_iota(jnp.int32, (rows, rows), 0) < lax.broadcasted_iota(
        jnp.int32, (rows, rows), 1
    )
    rank = jnp.dot(
        member.astype(jnp.float32).astype(jnp.bfloat16),
        before.astype(jnp.float32).astype(jnp.bfloat16),
        preferred_element_type=jnp.float32,
    )
    return jnp.where(member, rank, -1.0)


def dispatch_kernel(first, ids_hbm, tokens_hbm, out_ref, ids_ref, tokens_ref, code_ref, sem):
    part, count, width = out_ref.shape
    step = pl.program_id(0)

    @pl.when(step == 0)
    def _():
        load_ids = pltpu.make_async_copy(ids_hbm, ids_ref, sem.at[0])
        load_tokens = pltpu.make_async_copy(tokens_hbm, tokens_ref, sem.at[1])
        load_ids.start()
        load_tokens.start()
        load_ids.wait()
        code_ref[...] = slot_codes(ids_ref[...], code_ref.shape[0])
        load_tokens.wait()

    code = code_ref[pl.ds(pl.multiple_of(step * part, part), part), :]
    rows = code.shape[1]
    slots = first + lax.broadcasted_iota(jnp.int32, (part, count, rows), 1)
    pick = jnp.where(code[:, None, :] == slots.astype(jnp.float32), 1.0, 0.0)
    pick = pick.reshape(part * count, rows).astype(jnp.bfloat16)
    picked = jnp.dot(pick, tokens_ref[...], preferred_element_type=jnp.float32)
    out_ref[...] = picked.reshape(out_ref.shape).astype(jnp.bfloat16)


def dispatch(ids_t, tokens, experts, first, count):
    rows, width = tokens.shape
    part = 32
    return pl.pallas_call(
        functools.partial(dispatch_kernel, first),
        out_shape=pltpu.HBM((experts, count, width), jnp.bfloat16),
        grid=(experts // part,),
        in_specs=[pl.BlockSpec(memory_space=pltpu.HBM)] * 2,
        out_specs=pl.BlockSpec((part, count, width), lambda i: (i, 0, 0)),
        scratch_shapes=[
            pltpu.VMEM(ids_t.shape, ids_t.dtype),
            pltpu.VMEM((rows, width), tokens.dtype),
            pltpu.VMEM((experts, rows), jnp.float32),
            pltpu.SemaphoreType.DMA((2,)),
        ],
        compiler_params=pltpu.CompilerParams(vmem_limit_bytes=32 << 20),
        cost_estimate=pl.CostEstimate(
            flops=2 * experts * count * rows * width,
            bytes_accessed=2 * (experts * count + rows) * width,
            transcendentals=0,
        ),
        name="dispatch",
    )(
        pltpu.with_memory_space_constraint(ids_t, pltpu.HBM),
        pltpu.with_memory_space_constraint(tokens, pltpu.HBM),
    )


def ffn_kernel(rows_ref, weights_ref, out_ref):
    blocks, _, width_block, model = weights_ref.shape
    hidden_units = blocks * width_block
    contract_last = (((1,), (1,)), ((), ()))
    x = rows_ref[...]
    w_gate = weights_ref[:, 0].reshape(hidden_units, model)
    w_up = weights_ref[:, 1].reshape(hidden_units, model)
    w_down = weights_ref[:, 2].reshape(hidden_units, model)
    gate = lax.dot_general(x, w_gate, contract_last, preferred_element_type=jnp.float32)
    up = lax.dot_general(x, w_up, contract_last, preferred_element_type=jnp.float32)
    hidden = (gate / (1.0 + jnp.exp(-gate)) * up).astype(jnp.bfloat16)
    out_ref[...] = jnp.dot(hidden, w_down, preferred_element_type=jnp.float32).astype(jnp.bfloat16)


def expert_ffn(rows, weights):
    count, model = rows.shape
    part = 256
    return pl.pallas_call(
        ffn_kernel,
        out_shape=jax.ShapeDtypeStruct((count, model), jnp.bfloat16),
        grid=(count // part,),
        in_specs=[
            pl.BlockSpec((part, model), lambda i: (i, 0)),
            pl.BlockSpec(weights.shape, lambda i: (0, 0, 0, 0), pipeline_mode=pl.Buffered(1)),
        ],
        out_specs=pl.BlockSpec((part, model), lambda i: (i, 0)),
        compiler_params=pltpu.CompilerParams(vmem_limit_bytes=48 << 20),
        cost_estimate=pl.CostEstimate(
            flops=2 * count * weights.size,
            bytes_accessed=2 * (2 * rows.size + weights.size),
            transcendentals=count * weights.size // (3 * model),
        ),
        name="expert_ffn",
    )(rows, weights)


def coefficients_kernel(ids_ref, gates_ref, *out_refs):
    experts = out_refs[0].shape[1] // (MOST // len(out_refs))
    ids_t = ids_ref[...]
    rows = ids_t.shape[1]
    code = slot_codes(ids_t, experts)
    names = lax.broadcasted_iota(jnp.int32, (experts, rows), 0)
    gate = jnp.zeros((experts, rows), jnp.float32)
    for k in range(ids_t.shape[0]):
        gate = jnp.where(names == ids_t[k : k + 1, :], gates_ref[k : k + 1, :], gate)
    first = 0
    for out_ref in out_refs:
        count = out_ref.shape[1] // experts
        slots = first + lax.broadcasted_iota(jnp.int32, (experts, count, rows), 1)
        weight = jnp.where(code[:, None, :] == slots.astype(jnp.float32), gate[:, None, :], 0.0)
        weight = weight.reshape(experts * count, rows)
        high = weight.astype(jnp.bfloat16).astype(jnp.float32)
        out_ref[:rows, :] = high.T.astype(jnp.bfloat16)
        out_ref[rows:, :] = (weight - high).T.astype(jnp.bfloat16)
        first += count


def coefficients(ids_t, gates_t, experts, pieces):
    rows = ids_t.shape[1]
    width = experts * MOST // pieces
    return pl.pallas_call(
        coefficients_kernel,
        out_shape=[jax.ShapeDtypeStruct((2 * rows, width), jnp.bfloat16)] * pieces,
        compiler_params=pltpu.CompilerParams(vmem_limit_bytes=32 << 20),
        cost_estimate=pl.CostEstimate(
            flops=2 * experts * rows * rows,
            bytes_accessed=4 * rows * experts * MOST,
            transcendentals=0,
        ),
        name="coefficients",
    )(ids_t, gates_t)


def combine_kernel(weight_ref, values_ref, *refs):
    *start_refs, out_ref = refs
    rows = out_ref.shape[0]
    sums = jnp.dot(weight_ref[...], values_ref[...], preferred_element_type=jnp.float32)
    total = sums[:rows] + sums[rows:]
    if start_refs:
        total = start_refs[0][...] + total
    out_ref[...] = total.astype(out_ref.dtype)


def combine(weight, values, start, dtype):
    depth, width = values.shape
    rows = weight.shape[0] // 2
    part = 512
    column = pl.BlockSpec((rows, part), lambda i: (0, i))
    return pl.pallas_call(
        combine_kernel,
        out_shape=jax.ShapeDtypeStruct((rows, width), dtype),
        grid=(width // part,),
        in_specs=[
            pl.BlockSpec(weight.shape, lambda i: (0, 0)),
            pl.BlockSpec((depth, part), lambda i: (0, i)),
        ]
        + [column] * len(start),
        out_specs=column,
        compiler_params=pltpu.CompilerParams(vmem_limit_bytes=32 << 20),
        cost_estimate=pl.CostEstimate(
            flops=2 * weight.size * width,
            bytes_accessed=2 * (depth + rows) * width,
            transcendentals=0,
        ),
        name="combine",
    )(weight, values, *start)


def exchange(rows):
    return lax.all_to_all(rows, AXES, split_axis=0, concat_axis=0, tiled=True)


def body(tokens, expert_ids, route_gates, expert_weights):
    groups = lax.axis_size("expert")
    experts = expert_weights.shape[0] * groups
    model = tokens.shape[1]
    ids_t = expert_ids.T
    gates_t = route_gates.T
    half = MOST // 2
    out_a = dispatch(ids_t, tokens, experts, 0, half)
    out_b = dispatch(ids_t, tokens, experts, half, half)
    in_a = exchange(out_a)
    in_a, out_b, expert_weights = lax.optimization_barrier((in_a, out_b, expert_weights))
    weights = lax.all_to_all(expert_weights, "tensor", split_axis=0, concat_axis=0, tiled=True)
    in_a, out_b, weights = lax.optimization_barrier((in_a, out_b, weights))
    in_b = exchange(out_b)
    done_a = expert_ffn(in_a.reshape(experts * half, model), weights)
    done_a, in_b, ids_t, gates_t = lax.optimization_barrier((done_a, in_b, ids_t, gates_t))
    back_a = exchange(done_a.reshape(experts, half, model))
    done_b = expert_ffn(in_b.reshape(experts * half, model), weights)
    gates_a, gates_b = coefficients(ids_t, gates_t, experts, 2)
    done_b, back_a, gates_a, gates_b = lax.optimization_barrier(
        (done_b, back_a, gates_a, gates_b)
    )
    back_b = exchange(done_b.reshape(experts, half, model))
    part = combine(gates_a, back_a.reshape(experts * half, model), (), jnp.float32)
    return combine(gates_b, back_b.reshape(experts * half, model), (part,), jnp.bfloat16)


def solution(mesh):
    in_specs = (
        P(AXES, None),
        P(AXES, None),
        P(AXES, None),
        P("expert", None, "tensor", None),
    )
    return jax.shard_map(
        body, mesh=mesh, in_specs=in_specs, out_specs=P(AXES, None), check_vma=False
    )
```

```python
import functools

import jax
import jax.numpy as jnp
from jax import lax
from jax.experimental import pallas as pl
from jax.experimental.pallas import tpu as pltpu
from jax.sharding import PartitionSpec as P

MOST = 16
AXES = ("expert", "tensor")


def slot_codes(ids_t, experts):
    top, rows = ids_t.shape
    names = lax.broadcasted_iota(jnp.int32, (experts, rows), 0)
    member = names == ids_t[0:1, :]
    for k in range(1, top):
        member = member | (names == ids_t[k : k + 1, :])
    before = lax.broadcasted_iota(jnp.int32, (rows, rows), 0) < lax.broadcasted_iota(
        jnp.int32, (rows, rows), 1
    )
    rank = jnp.dot(
        member.astype(jnp.float32).astype(jnp.bfloat16),
        before.astype(jnp.float32).astype(jnp.bfloat16),
        preferred_element_type=jnp.float32,
    )
    return jnp.where(member, rank, -1.0)


def dispatch_kernel(first, ids_hbm, tokens_hbm, out_ref, ids_ref, tokens_ref, code_ref, sem):
    part, count, width = out_ref.shape
    step = pl.program_id(0)

    @pl.when(step == 0)
    def _():
        load_ids = pltpu.make_async_copy(ids_hbm, ids_ref, sem.at[0])
        load_tokens = pltpu.make_async_copy(tokens_hbm, tokens_ref, sem.at[1])
        load_ids.start()
        load_tokens.start()
        load_ids.wait()
        code_ref[...] = slot_codes(ids_ref[...], code_ref.shape[0])
        load_tokens.wait()

    code = code_ref[pl.ds(pl.multiple_of(step * part, part), part), :]
    rows = code.shape[1]
    slots = first + lax.broadcasted_iota(jnp.int32, (part, count, rows), 1)
    pick = jnp.where(code[:, None, :] == slots.astype(jnp.float32), 1.0, 0.0)
    pick = pick.reshape(part * count, rows).astype(jnp.bfloat16)
    picked = jnp.dot(pick, tokens_ref[...], preferred_element_type=jnp.float32)
    out_ref[...] = picked.reshape(out_ref.shape).astype(jnp.bfloat16)


def dispatch(ids_t, tokens, experts, first, count):
    rows, width = tokens.shape
    part = 64
    return pl.pallas_call(
        functools.partial(dispatch_kernel, first),
        out_shape=pltpu.HBM((experts, count, width), jnp.bfloat16),
        grid=(experts // part,),
        in_specs=[pl.BlockSpec(memory_space=pltpu.HBM)] * 2,
        out_specs=pl.BlockSpec((part, count, width), lambda i: (i, 0, 0)),
        scratch_shapes=[
            pltpu.VMEM(ids_t.shape, ids_t.dtype),
            pltpu.VMEM((rows, width), tokens.dtype),
            pltpu.VMEM((experts, rows), jnp.float32),
            pltpu.SemaphoreType.DMA((2,)),
        ],
        compiler_params=pltpu.CompilerParams(vmem_limit_bytes=32 << 20),
        cost_estimate=pl.CostEstimate(
            flops=2 * experts * count * rows * width,
            bytes_accessed=2 * (experts * count + rows) * width,
            transcendentals=0,
        ),
        name="dispatch",
    )(
        pltpu.with_memory_space_constraint(ids_t, pltpu.HBM),
        pltpu.with_memory_space_constraint(tokens, pltpu.HBM),
    )


def ffn_kernel(rows_ref, weights_ref, out_ref):
    blocks, _, width_block, model = weights_ref.shape
    hidden_units = blocks * width_block
    contract_last = (((1,), (1,)), ((), ()))
    x = rows_ref[...]
    w_gate = weights_ref[:, 0].reshape(hidden_units, model)
    w_up = weights_ref[:, 1].reshape(hidden_units, model)
    w_down = weights_ref[:, 2].reshape(hidden_units, model)
    gate = lax.dot_general(x, w_gate, contract_last, preferred_element_type=jnp.float32)
    up = lax.dot_general(x, w_up, contract_last, preferred_element_type=jnp.float32)
    hidden = (gate / (1.0 + jnp.exp(-gate)) * up).astype(jnp.bfloat16)
    out_ref[...] = jnp.dot(hidden, w_down, preferred_element_type=jnp.float32).astype(jnp.bfloat16)


def expert_ffn(rows, weights):
    count, model = rows.shape
    part = 256
    return pl.pallas_call(
        ffn_kernel,
        out_shape=jax.ShapeDtypeStruct((count, model), jnp.bfloat16),
        grid=(count // part,),
        in_specs=[
            pl.BlockSpec((part, model), lambda i: (i, 0)),
            pl.BlockSpec(weights.shape, lambda i: (0, 0, 0, 0), pipeline_mode=pl.Buffered(1)),
        ],
        out_specs=pl.BlockSpec((part, model), lambda i: (i, 0)),
        compiler_params=pltpu.CompilerParams(vmem_limit_bytes=48 << 20),
        cost_estimate=pl.CostEstimate(
            flops=2 * count * weights.size,
            bytes_accessed=2 * (2 * rows.size + weights.size),
            transcendentals=count * weights.size // (3 * model),
        ),
        name="expert_ffn",
    )(rows, weights)


def coefficients_kernel(ids_ref, gates_ref, *out_refs):
    experts = out_refs[0].shape[1] // (MOST // len(out_refs))
    ids_t = ids_ref[...]
    rows = ids_t.shape[1]
    code = slot_codes(ids_t, experts)
    names = lax.broadcasted_iota(jnp.int32, (experts, rows), 0)
    gate = jnp.zeros((experts, rows), jnp.float32)
    for k in range(ids_t.shape[0]):
        gate = jnp.where(names == ids_t[k : k + 1, :], gates_ref[k : k + 1, :], gate)
    first = 0
    for out_ref in out_refs:
        count = out_ref.shape[1] // experts
        slots = first + lax.broadcasted_iota(jnp.int32, (experts, count, rows), 1)
        weight = jnp.where(code[:, None, :] == slots.astype(jnp.float32), gate[:, None, :], 0.0)
        weight = weight.reshape(experts * count, rows)
        high = weight.astype(jnp.bfloat16).astype(jnp.float32)
        out_ref[:rows, :] = high.T.astype(jnp.bfloat16)
        out_ref[rows:, :] = (weight - high).T.astype(jnp.bfloat16)
        first += count


def coefficients(ids_t, gates_t, experts, pieces):
    rows = ids_t.shape[1]
    width = experts * MOST // pieces
    return pl.pallas_call(
        coefficients_kernel,
        out_shape=[jax.ShapeDtypeStruct((2 * rows, width), jnp.bfloat16)] * pieces,
        compiler_params=pltpu.CompilerParams(vmem_limit_bytes=32 << 20),
        cost_estimate=pl.CostEstimate(
            flops=2 * experts * rows * rows,
            bytes_accessed=4 * rows * experts * MOST,
            transcendentals=0,
        ),
        name="coefficients",
    )(ids_t, gates_t)


def combine_kernel(weight_ref, values_ref, *refs):
    *start_refs, out_ref = refs
    rows = out_ref.shape[0]
    sums = jnp.dot(weight_ref[...], values_ref[...], preferred_element_type=jnp.float32)
    total = sums[:rows] + sums[rows:]
    if start_refs:
        total = start_refs[0][...] + total
    out_ref[...] = total.astype(out_ref.dtype)


def combine(weight, values, start, dtype):
    depth, width = values.shape
    rows = weight.shape[0] // 2
    part = 1024
    column = pl.BlockSpec((rows, part), lambda i: (0, i))
    return pl.pallas_call(
        combine_kernel,
        out_shape=jax.ShapeDtypeStruct((rows, width), dtype),
        grid=(width // part,),
        in_specs=[
            pl.BlockSpec(weight.shape, lambda i: (0, 0)),
            pl.BlockSpec((depth, part), lambda i: (0, i)),
        ]
        + [column] * len(start),
        out_specs=column,
        compiler_params=pltpu.CompilerParams(vmem_limit_bytes=32 << 20),
        cost_estimate=pl.CostEstimate(
            flops=2 * weight.size * width,
            bytes_accessed=2 * (depth + rows) * width,
            transcendentals=0,
        ),
        name="combine",
    )(weight, values, *start)


def exchange(rows):
    return lax.all_to_all(rows, AXES, split_axis=0, concat_axis=0, tiled=True)


def body(tokens, expert_ids, route_gates, expert_weights):
    groups = lax.axis_size("expert")
    experts = expert_weights.shape[0] * groups
    model = tokens.shape[1]
    ids_t = expert_ids.T
    gates_t = route_gates.T
    half = MOST // 2
    out_a = dispatch(ids_t, tokens, experts, 0, half)
    out_b = dispatch(ids_t, tokens, experts, half, half)
    in_a = exchange(out_a)
    in_a, out_b, expert_weights = lax.optimization_barrier((in_a, out_b, expert_weights))
    weights = lax.all_to_all(expert_weights, "tensor", split_axis=0, concat_axis=0, tiled=True)
    in_a, out_b, weights = lax.optimization_barrier((in_a, out_b, weights))
    in_b = exchange(out_b)
    done_a = expert_ffn(in_a.reshape(experts * half, model), weights)
    done_a, in_b, ids_t, gates_t = lax.optimization_barrier((done_a, in_b, ids_t, gates_t))
    back_a = exchange(done_a.reshape(experts, half, model))
    done_b = expert_ffn(in_b.reshape(experts * half, model), weights)
    gates_a, gates_b = coefficients(ids_t, gates_t, experts, 2)
    done_b, back_a, gates_a, gates_b = lax.optimization_barrier(
        (done_b, back_a, gates_a, gates_b)
    )
    back_b = exchange(done_b.reshape(experts, half, model))
    part = combine(gates_a, back_a.reshape(experts * half, model), (), jnp.float32)
    return combine(gates_b, back_b.reshape(experts * half, model), (part,), jnp.bfloat16)


def solution(mesh):
    in_specs = (
        P(AXES, None),
        P(AXES, None),
        P(AXES, None),
        P("expert", None, "tensor", None),
    )
    return jax.shard_map(
        body, mesh=mesh, in_specs=in_specs, out_specs=P(AXES, None), check_vma=False
    )
```

```python
import functools

import jax
import jax.numpy as jnp
from jax import lax
from jax.experimental import pallas as pl
from jax.experimental.pallas import tpu as pltpu
from jax.sharding import PartitionSpec as P

MOST = 16
AXES = ("expert", "tensor")


def slot_codes(ids_t, experts):
    top, rows = ids_t.shape
    names = lax.broadcasted_iota(jnp.int32, (experts, rows), 0)
    member = names == ids_t[0:1, :]
    for k in range(1, top):
        member = member | (names == ids_t[k : k + 1, :])
    before = lax.broadcasted_iota(jnp.int32, (rows, rows), 0) < lax.broadcasted_iota(
        jnp.int32, (rows, rows), 1
    )
    rank = jnp.dot(
        member.astype(jnp.float32).astype(jnp.bfloat16),
        before.astype(jnp.float32).astype(jnp.bfloat16),
        preferred_element_type=jnp.float32,
    )
    return jnp.where(member, rank, -1.0)


def dispatch_kernel(first, ids_hbm, tokens_hbm, out_ref, ids_ref, tokens_ref, code_ref, sem):
    part, count, width = out_ref.shape
    step = pl.program_id(0)

    @pl.when(step == 0)
    def _():
        load_ids = pltpu.make_async_copy(ids_hbm, ids_ref, sem.at[0])
        load_tokens = pltpu.make_async_copy(tokens_hbm, tokens_ref, sem.at[1])
        load_ids.start()
        load_tokens.start()
        load_ids.wait()
        code_ref[...] = slot_codes(ids_ref[...], code_ref.shape[0])
        load_tokens.wait()

    code = code_ref[pl.ds(pl.multiple_of(step * part, part), part), :]
    rows = code.shape[1]
    slots = first + lax.broadcasted_iota(jnp.int32, (part, count, rows), 1)
    pick = jnp.where(code[:, None, :] == slots.astype(jnp.float32), 1.0, 0.0)
    pick = pick.reshape(part * count, rows).astype(jnp.bfloat16)
    picked = jnp.dot(pick, tokens_ref[...], preferred_element_type=jnp.float32)
    out_ref[...] = picked.reshape(out_ref.shape).astype(jnp.bfloat16)


def dispatch(ids_t, tokens, experts, first, count):
    rows, width = tokens.shape
    part = 64
    return pl.pallas_call(
        functools.partial(dispatch_kernel, first),
        out_shape=jax.ShapeDtypeStruct((experts, count, width), jnp.bfloat16),
        grid=(experts // part,),
        in_specs=[pl.BlockSpec(memory_space=pltpu.HBM)] * 2,
        out_specs=pl.BlockSpec((part, count, width), lambda i: (i, 0, 0)),
        scratch_shapes=[
            pltpu.VMEM(ids_t.shape, ids_t.dtype),
            pltpu.VMEM((rows, width), tokens.dtype),
            pltpu.VMEM((experts, rows), jnp.float32),
            pltpu.SemaphoreType.DMA((2,)),
        ],
        compiler_params=pltpu.CompilerParams(vmem_limit_bytes=32 << 20),
        cost_estimate=pl.CostEstimate(
            flops=2 * experts * count * rows * width,
            bytes_accessed=2 * (experts * count + rows) * width,
            transcendentals=0,
        ),
        name="dispatch",
    )(
        pltpu.with_memory_space_constraint(ids_t, pltpu.HBM),
        pltpu.with_memory_space_constraint(tokens, pltpu.HBM),
    )


def ffn_kernel(first, rows_ref, weights_ref, out_hbm, held, sem):
    blocks, _, width_block, model = weights_ref.shape
    hidden_units = blocks * width_block
    _, part, count, _ = held.shape
    contract_last = (((1,), (1,)), ((), ()))
    w_gate = weights_ref[:, 0].reshape(hidden_units, model)
    w_up = weights_ref[:, 1].reshape(hidden_units, model)
    w_down = weights_ref[:, 2].reshape(hidden_units, model)
    writes = []
    for tile in range(rows_ref.shape[0] // part):
        here = pl.ds(tile * part, part)
        x = rows_ref[here, first : first + count, :].reshape(part * count, model)
        gate = lax.dot_general(x, w_gate, contract_last, preferred_element_type=jnp.float32)
        up = lax.dot_general(x, w_up, contract_last, preferred_element_type=jnp.float32)
        hidden = (gate / (1.0 + jnp.exp(-gate)) * up).astype(jnp.bfloat16)
        out = jnp.dot(hidden, w_down, preferred_element_type=jnp.float32).astype(jnp.bfloat16)
        held[tile] = out.reshape(part, count, model)
        writes.append(pltpu.make_async_copy(held.at[tile], out_hbm.at[here], sem.at[tile]))
        writes[-1].start()
    for write in writes:
        write.wait()


def expert_ffn(arrived, weights, first, count):
    sources, _, model = arrived.shape
    part = 256 // count
    tiles = sources // part
    rows = sources * count
    return pl.pallas_call(
        functools.partial(ffn_kernel, first),
        out_shape=pltpu.HBM((sources, count, model), jnp.bfloat16),
        in_specs=[pl.BlockSpec(memory_space=pltpu.VMEM)] * 2,
        out_specs=pl.BlockSpec(memory_space=pltpu.HBM),
        scratch_shapes=[
            pltpu.VMEM((tiles, part, count, model), jnp.bfloat16),
            pltpu.SemaphoreType.DMA((tiles,)),
        ],
        compiler_params=pltpu.CompilerParams(vmem_limit_bytes=32 << 20),
        cost_estimate=pl.CostEstimate(
            flops=2 * rows * weights.size,
            bytes_accessed=2 * (2 * rows * model + weights.size),
            transcendentals=rows * weights.size // (3 * model),
        ),
        name="expert_ffn",
    )(arrived, weights)


def coefficients_kernel(ids_ref, gates_ref, *out_refs):
    experts = out_refs[0].shape[1] // (MOST // len(out_refs))
    ids_t = ids_ref[...]
    rows = ids_t.shape[1]
    code = slot_codes(ids_t, experts)
    names = lax.broadcasted_iota(jnp.int32, (experts, rows), 0)
    gate = jnp.zeros((experts, rows), jnp.float32)
    for k in range(ids_t.shape[0]):
        gate = jnp.where(names == ids_t[k : k + 1, :], gates_ref[k : k + 1, :], gate)
    first = 0
    for out_ref in out_refs:
        count = out_ref.shape[1] // experts
        slots = first + lax.broadcasted_iota(jnp.int32, (experts, count, rows), 1)
        weight = jnp.where(code[:, None, :] == slots.astype(jnp.float32), gate[:, None, :], 0.0)
        weight = weight.reshape(experts * count, rows)
        high = weight.astype(jnp.bfloat16).astype(jnp.float32)
        out_ref[:rows, :] = high.T.astype(jnp.bfloat16)
        out_ref[rows:, :] = (weight - high).T.astype(jnp.bfloat16)
        first += count


def coefficients(ids_t, gates_t, experts, pieces):
    rows = ids_t.shape[1]
    width = experts * MOST // pieces
    return pl.pallas_call(
        coefficients_kernel,
        out_shape=[jax.ShapeDtypeStruct((2 * rows, width), jnp.bfloat16)] * pieces,
        compiler_params=pltpu.CompilerParams(vmem_limit_bytes=32 << 20),
        cost_estimate=pl.CostEstimate(
            flops=2 * experts * rows * rows,
            bytes_accessed=4 * rows * experts * MOST,
            transcendentals=0,
        ),
        name="coefficients",
    )(ids_t, gates_t)


def combine_kernel(weight_ref, values_ref, *refs):
    *start_refs, out_ref = refs
    rows = out_ref.shape[0]
    sums = jnp.dot(weight_ref[...], values_ref[...], preferred_element_type=jnp.float32)
    total = sums[:rows] + sums[rows:]
    if start_refs:
        total = start_refs[0][...] + total
    out_ref[...] = total.astype(out_ref.dtype)


def combine(weight, values, start, dtype):
    depth, width = values.shape
    rows = weight.shape[0] // 2
    part = 1024
    column = pl.BlockSpec((rows, part), lambda i: (0, i))
    return pl.pallas_call(
        combine_kernel,
        out_shape=jax.ShapeDtypeStruct((rows, width), dtype),
        grid=(width // part,),
        in_specs=[
            pl.BlockSpec(weight.shape, lambda i: (0, 0)),
            pl.BlockSpec((depth, part), lambda i: (0, i)),
        ]
        + [column] * len(start),
        out_specs=column,
        compiler_params=pltpu.CompilerParams(vmem_limit_bytes=32 << 20),
        cost_estimate=pl.CostEstimate(
            flops=2 * weight.size * width,
            bytes_accessed=2 * (depth + rows) * width,
            transcendentals=0,
        ),
        name="combine",
    )(weight, values, *start)


def exchange(rows):
    return lax.all_to_all(rows, AXES, split_axis=0, concat_axis=0, tiled=True)


def body(tokens, expert_ids, route_gates, expert_weights):
    groups = lax.axis_size("expert")
    experts = expert_weights.shape[0] * groups
    model = tokens.shape[1]
    ids_t = expert_ids.T
    gates_t = route_gates.T
    half = MOST // 2
    outgoing = dispatch(ids_t, tokens, experts, 0, MOST)
    outgoing, expert_weights = lax.optimization_barrier((outgoing, expert_weights))
    weights = lax.all_to_all(expert_weights, "tensor", split_axis=0, concat_axis=0, tiled=True)
    outgoing, weights = lax.optimization_barrier((outgoing, weights))
    arrived = exchange(outgoing)
    done_a = expert_ffn(arrived, weights, 0, half)
    done_a, ids_t, gates_t = lax.optimization_barrier((done_a, ids_t, gates_t))
    back_a = exchange(done_a)
    done_b = expert_ffn(arrived, weights, half, half)
    gates_a, gates_b = coefficients(ids_t, gates_t, experts, 2)
    done_b, back_a, gates_a, gates_b = lax.optimization_barrier(
        (done_b, back_a, gates_a, gates_b)
    )
    back_b = exchange(done_b)
    part = combine(gates_a, back_a.reshape(experts * half, model), (), jnp.float32)
    return combine(gates_b, back_b.reshape(experts * half, model), (part,), jnp.bfloat16)


def solution(mesh):
    in_specs = (
        P(AXES, None),
        P(AXES, None),
        P(AXES, None),
        P("expert", None, "tensor", None),
    )
    return jax.shard_map(
        body, mesh=mesh, in_specs=in_specs, out_specs=P(AXES, None), check_vma=False
    )
```

```python
import functools

import jax
import jax.numpy as jnp
from jax import lax
from jax.experimental import pallas as pl
from jax.experimental.pallas import tpu as pltpu
from jax.sharding import PartitionSpec as P

MOST = 16
TILE = 256
AXES = ("expert", "tensor")


def slot_codes(ids_t, experts):
    top, rows = ids_t.shape
    names = lax.broadcasted_iota(jnp.int32, (experts, rows), 0)
    member = names == ids_t[0:1, :]
    for k in range(1, top):
        member = member | (names == ids_t[k : k + 1, :])
    before = lax.broadcasted_iota(jnp.int32, (rows, rows), 0) < lax.broadcasted_iota(
        jnp.int32, (rows, rows), 1
    )
    rank = jnp.dot(
        member.astype(jnp.float32).astype(jnp.bfloat16),
        before.astype(jnp.float32).astype(jnp.bfloat16),
        preferred_element_type=jnp.float32,
    )
    return jnp.where(member, rank, -1.0)


def dispatch_kernel(first, ids_hbm, tokens_hbm, out_ref, ids_ref, tokens_ref, code_ref, sem):
    part, count, width = out_ref.shape
    step = pl.program_id(0)

    @pl.when(step == 0)
    def _():
        load_ids = pltpu.make_async_copy(ids_hbm, ids_ref, sem.at[0])
        load_tokens = pltpu.make_async_copy(tokens_hbm, tokens_ref, sem.at[1])
        load_ids.start()
        load_tokens.start()
        load_ids.wait()
        code_ref[...] = slot_codes(ids_ref[...], code_ref.shape[0])
        load_tokens.wait()

    code = code_ref[pl.ds(pl.multiple_of(step * part, part), part), :]
    rows = code.shape[1]
    slots = first + lax.broadcasted_iota(jnp.int32, (part, count, rows), 1)
    pick = jnp.where(code[:, None, :] == slots.astype(jnp.float32), 1.0, 0.0)
    pick = pick.reshape(part * count, rows).astype(jnp.bfloat16)
    picked = jnp.dot(pick, tokens_ref[...], preferred_element_type=jnp.float32)
    out_ref[...] = picked.reshape(out_ref.shape).astype(jnp.bfloat16)


def dispatch(ids_t, tokens, experts, first, count):
    rows, width = tokens.shape
    part = 64
    return pl.pallas_call(
        functools.partial(dispatch_kernel, first),
        out_shape=jax.ShapeDtypeStruct((experts, count, width), jnp.bfloat16),
        grid=(experts // part,),
        in_specs=[pl.BlockSpec(memory_space=pltpu.HBM)] * 2,
        out_specs=pl.BlockSpec((part, count, width), lambda i: (i, 0, 0)),
        scratch_shapes=[
            pltpu.VMEM(ids_t.shape, ids_t.dtype),
            pltpu.VMEM((rows, width), tokens.dtype),
            pltpu.VMEM((experts, rows), jnp.float32),
            pltpu.SemaphoreType.DMA((2,)),
        ],
        compiler_params=pltpu.CompilerParams(vmem_limit_bytes=32 << 20),
        cost_estimate=pl.CostEstimate(
            flops=2 * experts * count * rows * width,
            bytes_accessed=2 * (experts * count + rows) * width,
            transcendentals=0,
        ),
        name="dispatch",
    )(
        pltpu.with_memory_space_constraint(ids_t, pltpu.HBM),
        pltpu.with_memory_space_constraint(tokens, pltpu.HBM),
    )


def ffn_kernel(rows_ref, weights_ref, out_ref):
    blocks, _, width_block, model = weights_ref.shape
    hidden_units = blocks * width_block
    contract_last = (((1,), (1,)), ((), ()))
    w_gate = weights_ref[:, 0].reshape(hidden_units, model)
    w_up = weights_ref[:, 1].reshape(hidden_units, model)
    w_down = weights_ref[:, 2].reshape(hidden_units, model)
    for tile in range(rows_ref.shape[0] // TILE):
        here = pl.ds(tile * TILE, TILE)
        x = rows_ref[here, :]
        gate = lax.dot_general(x, w_gate, contract_last, preferred_element_type=jnp.float32)
        up = lax.dot_general(x, w_up, contract_last, preferred_element_type=jnp.float32)
        hidden = (gate / (1.0 + jnp.exp(-gate)) * up).astype(jnp.bfloat16)
        out = jnp.dot(hidden, w_down, preferred_element_type=jnp.float32)
        out_ref[here, :] = out.astype(jnp.bfloat16)


def expert_ffn(rows, weights):
    count, model = rows.shape
    return pl.pallas_call(
        ffn_kernel,
        out_shape=jax.ShapeDtypeStruct((count, model), jnp.bfloat16),
        in_specs=[pl.BlockSpec(memory_space=pltpu.VMEM)] * 2,
        out_specs=pl.BlockSpec(memory_space=pltpu.VMEM),
        compiler_params=pltpu.CompilerParams(vmem_limit_bytes=20 << 20),
        cost_estimate=pl.CostEstimate(
            flops=2 * count * weights.size,
            bytes_accessed=2 * (2 * rows.size + weights.size),
            transcendentals=count * weights.size // (3 * model),
        ),
        name="expert_ffn",
    )(rows, weights)


def coefficients_kernel(ids_ref, gates_ref, *out_refs):
    experts = out_refs[0].shape[1] // (MOST // len(out_refs))
    ids_t = ids_ref[...]
    rows = ids_t.shape[1]
    code = slot_codes(ids_t, experts)
    names = lax.broadcasted_iota(jnp.int32, (experts, rows), 0)
    gate = jnp.zeros((experts, rows), jnp.float32)
    for k in range(ids_t.shape[0]):
        gate = jnp.where(names == ids_t[k : k + 1, :], gates_ref[k : k + 1, :], gate)
    first = 0
    for out_ref in out_refs:
        count = out_ref.shape[1] // experts
        slots = first + lax.broadcasted_iota(jnp.int32, (experts, count, rows), 1)
        weight = jnp.where(code[:, None, :] == slots.astype(jnp.float32), gate[:, None, :], 0.0)
        weight = weight.reshape(experts * count, rows)
        high = weight.astype(jnp.bfloat16).astype(jnp.float32)
        out_ref[:rows, :] = high.T.astype(jnp.bfloat16)
        out_ref[rows:, :] = (weight - high).T.astype(jnp.bfloat16)
        first += count


def coefficients(ids_t, gates_t, experts, pieces):
    rows = ids_t.shape[1]
    width = experts * MOST // pieces
    return pl.pallas_call(
        coefficients_kernel,
        out_shape=[jax.ShapeDtypeStruct((2 * rows, width), jnp.bfloat16)] * pieces,
        compiler_params=pltpu.CompilerParams(vmem_limit_bytes=32 << 20),
        cost_estimate=pl.CostEstimate(
            flops=2 * experts * rows * rows,
            bytes_accessed=4 * rows * experts * MOST,
            transcendentals=0,
        ),
        name="coefficients",
    )(ids_t, gates_t)


def combine_kernel(weight_ref, values_ref, out_ref):
    rows, width = out_ref.shape
    part = 512
    for first in range(0, width, part):
        here = pl.ds(first, part)
        sums = jnp.dot(
            weight_ref[...], values_ref[:, here], preferred_element_type=jnp.float32
        )
        out_ref[:, here] = (sums[:rows] + sums[rows:]).astype(out_ref.dtype)


def combine(weight, values):
    depth, width = values.shape
    rows = weight.shape[0] // 2
    return pl.pallas_call(
        combine_kernel,
        out_shape=jax.ShapeDtypeStruct((rows, width), jnp.bfloat16),
        in_specs=[pl.BlockSpec(memory_space=pltpu.VMEM)] * 2,
        out_specs=pl.BlockSpec(memory_space=pltpu.VMEM),
        compiler_params=pltpu.CompilerParams(vmem_limit_bytes=16 << 20),
        cost_estimate=pl.CostEstimate(
            flops=2 * weight.size * width,
            bytes_accessed=2 * (depth + rows) * width,
            transcendentals=0,
        ),
        name="combine",
    )(weight, values)


def exchange(rows):
    return lax.all_to_all(rows, AXES, split_axis=0, concat_axis=0, tiled=True)


def body(tokens, expert_ids, route_gates, expert_weights):
    groups = lax.axis_size("expert")
    experts = expert_weights.shape[0] * groups
    model = tokens.shape[1]
    ids_t = expert_ids.T
    gates_t = route_gates.T
    outgoing = dispatch(ids_t, tokens, experts, 0, MOST)
    outgoing, expert_weights = lax.optimization_barrier((outgoing, expert_weights))
    weights = lax.all_to_all(expert_weights, "tensor", split_axis=0, concat_axis=0, tiled=True)
    outgoing, weights = lax.optimization_barrier((outgoing, weights))
    arrived = exchange(outgoing)
    arrived, ids_t, gates_t = lax.optimization_barrier((arrived, ids_t, gates_t))
    (gates,) = coefficients(ids_t, gates_t, experts, 1)
    outputs = expert_ffn(arrived.reshape(experts * MOST, model), weights)
    outputs, gates = lax.optimization_barrier((outputs, gates))
    returned = exchange(outputs.reshape(experts, MOST, model))
    return combine(gates, returned.reshape(experts * MOST, model))


def solution(mesh):
    in_specs = (
        P(AXES, None),
        P(AXES, None),
        P(AXES, None),
        P("expert", None, "tensor", None),
    )
    return jax.shard_map(
        body, mesh=mesh, in_specs=in_specs, out_specs=P(AXES, None), check_vma=False
    )
```

```python
import functools

import jax
import jax.numpy as jnp
from jax import lax
from jax.experimental import pallas as pl
from jax.experimental.pallas import tpu as pltpu
from jax.sharding import PartitionSpec as P

MOST = 16
TILE = 256
AXES = ("expert", "tensor")


def places(ids, grid):
    groups, tensors = grid
    return lax.rem(ids, tensors) * groups + lax.div(ids, tensors)


def slot_codes(ids_t, experts):
    top, rows = ids_t.shape
    names = lax.broadcasted_iota(jnp.int32, (experts, rows), 0)
    member = names == ids_t[0:1, :]
    for k in range(1, top):
        member = member | (names == ids_t[k : k + 1, :])
    before = lax.broadcasted_iota(jnp.int32, (rows, rows), 0) < lax.broadcasted_iota(
        jnp.int32, (rows, rows), 1
    )
    rank = jnp.dot(
        member.astype(jnp.float32).astype(jnp.bfloat16),
        before.astype(jnp.float32).astype(jnp.bfloat16),
        preferred_element_type=jnp.float32,
    )
    return jnp.where(member, rank, -1.0)


def dispatch_kernel(first, grid, ids_hbm, tokens_hbm, out_ref, ids_ref, tokens_ref, code_ref, sem):
    part, count, width = out_ref.shape
    step = pl.program_id(0)

    @pl.when(step == 0)
    def _():
        load_ids = pltpu.make_async_copy(ids_hbm, ids_ref, sem.at[0])
        load_tokens = pltpu.make_async_copy(tokens_hbm, tokens_ref, sem.at[1])
        load_ids.start()
        load_tokens.start()
        load_ids.wait()
        code_ref[...] = slot_codes(places(ids_ref[...], grid), code_ref.shape[0])
        load_tokens.wait()

    code = code_ref[pl.ds(pl.multiple_of(step * part, part), part), :]
    rows = code.shape[1]
    slots = first + lax.broadcasted_iota(jnp.int32, (part, count, rows), 1)
    pick = jnp.where(code[:, None, :] == slots.astype(jnp.float32), 1.0, 0.0)
    pick = pick.reshape(part * count, rows).astype(jnp.bfloat16)
    picked = jnp.dot(pick, tokens_ref[...], preferred_element_type=jnp.float32)
    out_ref[...] = picked.reshape(out_ref.shape).astype(jnp.bfloat16)


def dispatch(ids_t, tokens, experts, first, count, grid):
    rows, width = tokens.shape
    part = 64
    return pl.pallas_call(
        functools.partial(dispatch_kernel, first, grid),
        out_shape=jax.ShapeDtypeStruct((experts, count, width), jnp.bfloat16),
        grid=(experts // part,),
        in_specs=[pl.BlockSpec(memory_space=pltpu.HBM)] * 2,
        out_specs=pl.BlockSpec((part, count, width), lambda i: (i, 0, 0)),
        scratch_shapes=[
            pltpu.VMEM(ids_t.shape, ids_t.dtype),
            pltpu.VMEM((rows, width), tokens.dtype),
            pltpu.VMEM((experts, rows), jnp.float32),
            pltpu.SemaphoreType.DMA((2,)),
        ],
        compiler_params=pltpu.CompilerParams(vmem_limit_bytes=32 << 20),
        cost_estimate=pl.CostEstimate(
            flops=2 * experts * count * rows * width,
            bytes_accessed=2 * (experts * count + rows) * width,
            transcendentals=0,
        ),
        name="dispatch",
    )(
        pltpu.with_memory_space_constraint(ids_t, pltpu.HBM),
        pltpu.with_memory_space_constraint(tokens, pltpu.HBM),
    )


def ffn_kernel(rows_ref, weights_ref, out_ref):
    blocks, _, width_block, model = weights_ref.shape
    hidden_units = blocks * width_block
    contract_last = (((1,), (1,)), ((), ()))
    w_gate = weights_ref[:, 0].reshape(hidden_units, model)
    w_up = weights_ref[:, 1].reshape(hidden_units, model)
    w_down = weights_ref[:, 2].reshape(hidden_units, model)
    for tile in range(rows_ref.shape[0] // TILE):
        here = pl.ds(tile * TILE, TILE)
        x = rows_ref[here, :]
        gate = lax.dot_general(x, w_gate, contract_last, preferred_element_type=jnp.float32)
        up = lax.dot_general(x, w_up, contract_last, preferred_element_type=jnp.float32)
        hidden = (gate / (1.0 + jnp.exp(-gate)) * up).astype(jnp.bfloat16)
        out = jnp.dot(hidden, w_down, preferred_element_type=jnp.float32)
        out_ref[here, :] = out.astype(jnp.bfloat16)


def expert_ffn(rows, weights):
    count, model = rows.shape
    return pl.pallas_call(
        ffn_kernel,
        out_shape=jax.ShapeDtypeStruct((count, model), jnp.bfloat16),
        in_specs=[pl.BlockSpec(memory_space=pltpu.VMEM)] * 2,
        out_specs=pl.BlockSpec(memory_space=pltpu.VMEM),
        compiler_params=pltpu.CompilerParams(vmem_limit_bytes=20 << 20),
        cost_estimate=pl.CostEstimate(
            flops=2 * count * weights.size,
            bytes_accessed=2 * (2 * rows.size + weights.size),
            transcendentals=count * weights.size // (3 * model),
        ),
        name="expert_ffn",
    )(rows, weights)


def coefficients_kernel(grid, ids_ref, gates_ref, *out_refs):
    experts = out_refs[0].shape[1] // (MOST // len(out_refs))
    ids_t = places(ids_ref[...], grid)
    rows = ids_t.shape[1]
    code = slot_codes(ids_t, experts)
    names = lax.broadcasted_iota(jnp.int32, (experts, rows), 0)
    gate = jnp.zeros((experts, rows), jnp.float32)
    for k in range(ids_t.shape[0]):
        gate = jnp.where(names == ids_t[k : k + 1, :], gates_ref[k : k + 1, :], gate)
    first = 0
    for out_ref in out_refs:
        count = out_ref.shape[1] // experts
        slots = first + lax.broadcasted_iota(jnp.int32, (experts, count, rows), 1)
        weight = jnp.where(code[:, None, :] == slots.astype(jnp.float32), gate[:, None, :], 0.0)
        weight = weight.reshape(experts * count, rows)
        high = weight.astype(jnp.bfloat16).astype(jnp.float32)
        out_ref[:rows, :] = high.T.astype(jnp.bfloat16)
        out_ref[rows:, :] = (weight - high).T.astype(jnp.bfloat16)
        first += count


def coefficients(ids_t, gates_t, experts, pieces, grid):
    rows = ids_t.shape[1]
    width = experts * MOST // pieces
    return pl.pallas_call(
        functools.partial(coefficients_kernel, grid),
        out_shape=[jax.ShapeDtypeStruct((2 * rows, width), jnp.bfloat16)] * pieces,
        compiler_params=pltpu.CompilerParams(vmem_limit_bytes=32 << 20),
        cost_estimate=pl.CostEstimate(
            flops=2 * experts * rows * rows,
            bytes_accessed=4 * rows * experts * MOST,
            transcendentals=0,
        ),
        name="coefficients",
    )(ids_t, gates_t)


def combine_kernel(weight_ref, values_ref, out_ref):
    rows, width = out_ref.shape
    part = 512
    for first in range(0, width, part):
        here = pl.ds(first, part)
        sums = jnp.dot(
            weight_ref[...], values_ref[:, here], preferred_element_type=jnp.float32
        )
        out_ref[:, here] = (sums[:rows] + sums[rows:]).astype(out_ref.dtype)


def combine(weight, values):
    depth, width = values.shape
    rows = weight.shape[0] // 2
    return pl.pallas_call(
        combine_kernel,
        out_shape=jax.ShapeDtypeStruct((rows, width), jnp.bfloat16),
        in_specs=[pl.BlockSpec(memory_space=pltpu.VMEM)] * 2,
        out_specs=pl.BlockSpec(memory_space=pltpu.VMEM),
        compiler_params=pltpu.CompilerParams(vmem_limit_bytes=16 << 20),
        cost_estimate=pl.CostEstimate(
            flops=2 * weight.size * width,
            bytes_accessed=2 * (depth + rows) * width,
            transcendentals=0,
        ),
        name="combine",
    )(weight, values)


def exchange(rows):
    return lax.all_to_all(rows, ("tensor", "expert"), split_axis=0, concat_axis=0, tiled=True)


def body(tokens, expert_ids, route_gates, expert_weights):
    groups = lax.axis_size("expert")
    experts = expert_weights.shape[0] * groups
    model = tokens.shape[1]
    grid = (groups, lax.axis_size("tensor"))
    ids_t = expert_ids.T
    gates_t = route_gates.T
    outgoing = dispatch(ids_t, tokens, experts, 0, MOST, grid)
    outgoing, expert_weights = lax.optimization_barrier((outgoing, expert_weights))
    weights = lax.all_to_all(expert_weights, "tensor", split_axis=0, concat_axis=0, tiled=True)
    outgoing, weights = lax.optimization_barrier((outgoing, weights))
    arrived = exchange(outgoing)
    arrived, ids_t, gates_t = lax.optimization_barrier((arrived, ids_t, gates_t))
    (gates,) = coefficients(ids_t, gates_t, experts, 1, grid)
    outputs = expert_ffn(arrived.reshape(experts * MOST, model), weights)
    outputs, gates = lax.optimization_barrier((outputs, gates))
    returned = exchange(outputs.reshape(experts, MOST, model))
    return combine(gates, returned.reshape(experts * MOST, model))


def solution(mesh):
    in_specs = (
        P(AXES, None),
        P(AXES, None),
        P(AXES, None),
        P("expert", None, "tensor", None),
    )
    return jax.shard_map(
        body, mesh=mesh, in_specs=in_specs, out_specs=P(AXES, None), check_vma=False
    )
```
